512 devices in a mesh: dev: 128 (over x, z_lo, y, core), rep: 4 (over z_hi).
Axes of the slice: x: 4, y: 8, z: 8 (z_hi: 4, z_lo: 2; z = z_hi * 2 + z_lo), core: 2. Of those that a mesh axis runs over, the one named last changes fastest.
Arguments:
- backbone: bfloat16 [512, 16, 8, 512], P(('rep', 'dev')), parts along dimension 0, may hold values from -6 to 6
- conv_weight: bfloat16 [3, 3, 512, 2048], P(None, None, None, ('rep', 'dev')), parts along dimension 3, may hold values from -0.35355339 to 0.35355339
- smooth_weight: float32 [3, 3, 2048], P(None, None, 'rep'), parts along dimension 2, may hold values from -2.5 to 2.5
Outputs:
- smoothed: bfloat16 [512, 16, 8, 512], P(('rep', 'dev')), parts along dimension 0
The draws below stay inside these ranges and needn't reach their ends.
There are 4 independent parts, one for each index of `rep`. The reference program is written for one: setup_inputs(seed, part) draws one part's arguments, and reference() takes and returns one part's arrays. A program takes and returns all parts, laid end to end along the dimension named above; each array names one. Nothing has to cross between parts.
All inputs are finite; a program needn't handle non-finite values.
Results may differ from the reference program's by a relative error of at most 0.0073.
Values may be sent and summed in bfloat16 or wider, within the bound.
No kernel may reach another device: no remote copies, remote signals or barrier semaphores. Data moves between devices by JAX's collectives and lax.ppermute only.
A program may use at most 64 MiB of HBM per device.

```python
import jax
import jax.numpy as jnp
from jax import lax

C = 512
GRID_H = 16
GRID_W = 8
ITERS = 2
IMAGES = 128


def draw_conv_weight(key, part):
    base_key = jax.random.fold_in(key, 11)
    scale_key = jax.random.fold_in(key, 23)
    base = jnp.clip(jax.random.normal(base_key, (3, 3, C, C), jnp.float32), -6.0, 6.0)
    scales = jnp.exp(jax.random.uniform(scale_key, (C,), jnp.float32, jnp.log(0.3), jnp.log(3.0)))
    weights = base * scales / jnp.sqrt(9.0 * C)
    return weights.astype(jnp.bfloat16)


def block_levels(rng, dims, split, least, largest):
    gain = 1.0
    for axis_at, parts in split:
        steps = jax.random.uniform(jax.random.fold_in(jax.random.fold_in(rng, 6), axis_at), (parts,), jnp.float32, least / len(split), largest / len(split))
        gain = gain * jnp.repeat(jnp.exp(steps), dims[axis_at] // parts).reshape((-1,) + (1,) * (len(dims) - 1 - axis_at))
    return gain


def bell_draw(stream_key, shape, deviation, reach, split=(), kind=jnp.bfloat16):
    factor_of = block_levels(stream_key, shape, split, -0.22, 0.18) if split else 1.0
    values = jax.random.normal(stream_key, shape, jnp.float32) * deviation * factor_of
    return jnp.minimum(jnp.maximum(values, -reach), reach).astype(kind)


def setup_inputs(seed: int = 0, part: int = 0) -> dict:
    key_of = jax.random.split(jax.random.key(seed), 4)
    part_keys = jax.random.split(jax.random.fold_in(key_of[3], part), 4)
    return {
        "backbone": bell_draw(part_keys[0], (IMAGES, GRID_H, GRID_W, C), 1.0, 6.0, ((0, 128),)),
        "conv_weight": draw_conv_weight(jax.random.fold_in(jax.random.fold_in(key_of[3], part), 71), part),
        "smooth_weight": bell_draw(part_keys[2], (3, 3, C), 0.35, 2.5, (), jnp.float32),
    }


ridge_term = 0.5

def convolve(padded, weights, grid_rows, grid_cols):
    summed = None
    for row_tap in range(3):
        for col_tap in range(3):
            window = padded[:, row_tap:row_tap + grid_rows, col_tap:col_tap + grid_cols, :]
            flat_window = window.reshape(-1, window.shape[3])
            product = jnp.dot(flat_window, weights[row_tap, col_tap], preferred_element_type=jnp.float32)
            summed = product if summed is None else summed + product
    return summed.reshape(padded.shape[0], grid_rows, grid_cols, weights.shape[3])

def newton_root(moments):
    identity = jnp.eye(C, dtype=jnp.float32)
    frob = jnp.sqrt(jnp.sum(moments * moments))
    upper = moments / frob
    lower = identity
    for sweep in range(ITERS):
        product = jnp.dot(lower, upper, precision=lax.Precision.HIGHEST)
        factor = 1.5 * identity - 0.5 * product
        if sweep + 1 < ITERS:
            upper = jnp.dot(upper, factor, precision=lax.Precision.HIGHEST)
        lower = jnp.dot(factor, lower, precision=lax.Precision.HIGHEST)
    return lower / jnp.sqrt(frob)

def reference(backbone, conv_weight, smooth_weight):
    image_count = backbone.shape[0]
    padded = jnp.pad(backbone, ((0, 0), (1, 1), (1, 1), (0, 0)))
    features = convolve(padded, conv_weight, GRID_H, GRID_W).astype(jnp.bfloat16)
    columns = features.reshape(image_count, GRID_H * GRID_W, C).transpose(1, 0, 2)
    identity = jnp.eye(C, dtype=jnp.float32)

    def per_position(column):
        center = lax.optimization_barrier(jnp.sum(column.astype(jnp.float32), axis=0)) / image_count
        centered = (column.astype(jnp.float32) - center).astype(jnp.bfloat16)
        gram = jnp.dot(centered.T, centered, preferred_element_type=jnp.float32)
        moments = gram / (image_count - 1) + ridge_term * identity
        inverse_root = newton_root(moments).astype(jnp.bfloat16)
        return jnp.dot(centered, inverse_root, preferred_element_type=jnp.float32).astype(jnp.bfloat16)
    whitened = lax.map(per_position, columns)
    whitened = whitened.transpose(1, 0, 2).reshape(image_count, GRID_H, GRID_W, C)
    padded_white = jnp.pad(whitened, ((0, 0), (1, 1), (1, 1), (0, 0)))
    summed = jnp.zeros((image_count, GRID_H, GRID_W, C), jnp.float32)
    for row_tap in range(3):
        for col_tap in range(3):
            window = padded_white[:, row_tap:row_tap + GRID_H, col_tap:col_tap + GRID_W, :]
            summed = summed + window.astype(jnp.float32) * smooth_weight[row_tap, col_tap]
    return summed.astype(jnp.bfloat16)
```

```python
import numpy as np
import jax
import jax.numpy as jnp
from jax import lax
from jax.experimental import pallas as pl
from jax.experimental.pallas import tpu as pltpu
from jax.sharding import Mesh, PartitionSpec as P

ITERS = 2
RIDGE = 0.5
NX, NZ, NY, NC = 4, 2, 8, 2
ROWS, COLS, CH, IMAGES = 16, 8, 512, 128
F32, BF16 = jnp.float32, jnp.bfloat16
AXES = ("x", "z", "y", "c")
NT = (((1,), (1,)), ((), ()))


def vmem_call(body, out_shape, scratch, name):
    return pl.pallas_call(
        body,
        out_shape=out_shape,
        scratch_shapes=scratch,
        name=name,
        compiler_params=pltpu.CompilerParams(vmem_limit_bytes=48 * 1024 * 1024),
    )


def interleave_body(own_ref, partner_ref, out_ref, rows_ref):
    for t in range(4):
        lanes = slice(t * 128, (t + 1) * 128)
        for j in range(4):
            rows_ref[t, pl.ds(j, IMAGES, stride=8), :] = own_ref[j, :, lanes].astype(F32)
            rows_ref[t, pl.ds(4 + j, IMAGES, stride=8), :] = partner_ref[j, :, lanes].astype(F32)
        out_ref[:, lanes] = rows_ref[t].astype(BF16)


def conv_body(weight_ref, x_ref, out_ref, wide_ref, z_ref):
    taps, group = weight_ref.shape[1], weight_ref.shape[0]
    for t in range(taps):
        for g in range(group):
            at = t * 64 + g * 4
            wide_ref[at : at + 4, :] = weight_ref[g, t].astype(F32)
    wide_ref[576:640, :] = jnp.zeros((64, CH), F32)
    z_ref[0] = jnp.zeros((10, 8, 640), F32)
    z_ref[17] = jnp.zeros((10, 8, 640), F32)
    z_ref[:, 0] = jnp.zeros((18, 8, 640), F32)
    z_ref[:, 9] = jnp.zeros((18, 8, 640), F32)
    x = x_ref[...]
    for lo, hi in ((0, 256), (256, 512), (512, 640)):
        part = lax.dot_general(x, wide_ref[lo:hi, :].astype(BF16), NT, preferred_element_type=F32)
        z_ref[1:17, 1:9, :, lo:hi] = part.reshape(ROWS, COLS, 8, hi - lo)
    lane_lo = lax.broadcasted_iota(jnp.int32, (4, 8, 128), 2) < 64
    row_lo = lax.broadcasted_iota(jnp.int32, (4, 8, 128), 1) < 4
    for h in range(ROWS):
        sums = [None, None]
        for t in range(taps):
            a, b, tile = t // 3, t % 3, (t // 2) * 128
            piece = z_ref[h + a, b : b + 8, :, tile : tile + 128]
            sums[t % 2] = piece if sums[t % 2] is None else sums[t % 2] + piece
        total = sums[0] + pltpu.roll(sums[1], 64, 2)
        pairs = total.reshape(4, 2, 8, 128)
        even, odd = pairs[:, 0], pairs[:, 1]
        first = jnp.where(row_lo, even, pltpu.roll(odd, 4, 1))
        second = jnp.where(row_lo, pltpu.roll(even, 4, 1), odd)
        packed = jnp.where(lane_lo, first, pltpu.roll(second, 64, 2))
        out_ref[h * 32 : (h + 1) * 32, :] = packed.reshape(32, 128).astype(BF16)


def exact_dot(a, b):
    return jnp.dot(a, b, precision=lax.Precision.HIGHEST, preferred_element_type=F32)


def stats_body(got_ref, pick_ref, lanes_ref, out_ref, rows_ref):
    lane_lo = lax.broadcasted_iota(jnp.int32, (IMAGES, 128), 1) < 64
    even_row = lax.broadcasted_iota(jnp.int32, (IMAGES, 128), 0) % 2 == 0
    eye = (
        lax.broadcasted_iota(jnp.int32, (IMAGES, IMAGES), 0)
        == lax.broadcasted_iota(jnp.int32, (IMAGES, IMAGES), 1)
    ).astype(F32)
    centered = []
    gram = None
    for k in range(NX):
        block = got_ref[k * 128 : (k + 1) * 128, :]
        from0 = jnp.dot(pick_ref[2 * k], block, preferred_element_type=F32)
        from1 = jnp.dot(pick_ref[2 * k + 1], block, preferred_element_type=F32)
        same = jnp.where(lane_lo, from0, from1)
        swapped = pltpu.roll(jnp.where(lane_lo, from1, from0), 64, 1)
        mixed = jnp.where(even_row, same, swapped).astype(BF16)
        x = jnp.dot(mixed, lanes_ref[...], preferred_element_type=F32)
        center = jnp.sum(x, axis=0, keepdims=True) / IMAGES
        x = (x - center).astype(BF16)
        centered.append(x)
        part = lax.dot_general(x, x, NT, preferred_element_type=F32)
        gram = part if gram is None else gram + part
    scaled = gram / (IMAGES - 1)
    trace = jnp.sum(scaled * eye)
    frob = jnp.sqrt(jnp.sum(scaled * scaled) + 2.0 * RIDGE * trace + RIDGE * RIDGE * CH)
    upper = (scaled + RIDGE * eye) / frob
    lower = 1.5 * eye - 0.5 * upper
    upper = exact_dot(upper, lower)
    for sweep in range(1, ITERS):
        factor = 1.5 * eye - 0.5 * exact_dot(lower, upper)
        if sweep + 1 < ITERS:
            upper = exact_dot(upper, factor)
        lower = exact_dot(factor, lower)
    lower = lower / jnp.sqrt(frob)
    high = lower.astype(BF16)
    low = (lower - high.astype(F32)).astype(BF16)
    for k in range(NX):
        white = jnp.dot(high, centered[k], preferred_element_type=F32)
        white = white + jnp.dot(low, centered[k], preferred_element_type=F32)
        rows_ref[pl.ds(k, IMAGES, stride=4), :] = white
    out_ref[...] = rows_ref[...].astype(BF16)


def smooth_body(white_ref, weight_ref, out_ref, pad_ref, rows_ref):
    pad_ref[...] = jnp.zeros((18, 40, 128), F32)
    pad_ref[1:17, 4:36, :] = white_ref[...].astype(F32).reshape(ROWS, 32, 128)
    total = None
    for t in range(9):
        a, b = t // 3, t % 3
        piece = pad_ref[a : a + ROWS, 4 * b : 4 * b + 32, :] * weight_ref[t][None]
        total = piece if total is None else total + piece
    rows_ref[...] = total.reshape(512, 128)
    for k in range(NX):
        out_ref[:, k * 128 : (k + 1) * 128] = rows_ref[pl.ds(k, 128, stride=4), :].astype(BF16)


def pick_tables():
    picks = np.zeros((2 * NX, IMAGES, 128), np.float32)
    for x in range(NX):
        for c in range(NC):
            for n in range(IMAGES):
                xs, zy = n // 32, (n // 2) % 16
                picks[2 * x + c, n, zy * 8 + c * 4 + (x - xs) % NX] = 1.0
    lanes = np.zeros((128, 128), np.float32)
    for c in range(NC):
        for zy in range(16):
            for k in range(4):
                lanes[c * 64 + zy * 4 + k, zy * 8 + c * 4 + k] = 1.0
    return picks, lanes


PICKS, LANES = pick_tables()


def shards(backbone, conv_weight, smooth_weight):
    image = backbone.reshape(ROWS * COLS, CH)
    chunk = conv_weight.transpose(0, 1, 3, 2).reshape(9, 4, CH)
    spread = jnp.broadcast_to(chunk[None], (NZ * NY, 9, 4, CH))
    kernels = lax.all_to_all(spread, ("z", "y"), 0, 0, tiled=True)
    own = [image]
    for k in range(1, NX):
        own.append(lax.ppermute(image, "x", [(i, (i + k) % NX) for i in range(NX)]))
    own = jnp.stack(own)
    partner = lax.ppermute(own, "c", [(0, 1), (1, 0)])
    x = vmem_call(
        interleave_body,
        jax.ShapeDtypeStruct((1024, CH), BF16),
        [pltpu.VMEM((4, 1024, 128), F32)],
        "interleave",
    )(own, partner)
    features = vmem_call(
        conv_body,
        jax.ShapeDtypeStruct((512, 128), BF16),
        [pltpu.VMEM((640, CH), F32), pltpu.VMEM((18, 10, 8, 640), F32)],
        "conv",
    )(kernels, x)
    got = lax.all_to_all(features.reshape(128, 4, 128), AXES, 0, 0, tiled=True)
    white = vmem_call(
        stats_body,
        jax.ShapeDtypeStruct((512, 128), BF16),
        [pltpu.VMEM((512, 128), F32)],
        "stats",
    )(got.reshape(512, 128), jnp.asarray(PICKS, BF16), jnp.asarray(LANES, BF16))
    back = lax.all_to_all(white.reshape(128, 4, 128), AXES, 0, 0, tiled=True)
    taps = jnp.tile(smooth_weight.reshape(9, 4, 128), (1, 8, 1))
    out = vmem_call(
        smooth_body,
        jax.ShapeDtypeStruct((128, CH), BF16),
        [pltpu.VMEM((18, 40, 128), F32), pltpu.VMEM((512, 128), F32)],
        "smooth",
    )(back.reshape(512, 128), taps)
    return out.reshape(1, ROWS, COLS, CH)


def solution(mesh):
    split = Mesh(
        mesh.devices.reshape(NX, NZ, NY, NC, mesh.shape["rep"]), AXES + ("rep",)
    )
    whole = ("rep",) + AXES
    return jax.shard_map(
        shards,
        mesh=split,
        in_specs=(P(whole, None, None, None), P(None, None, None, whole), P(None, None, "rep")),
        out_specs=P(whole, None, None, None),
        check_vma=False,
    )
```

```python
import numpy as np
import jax
import jax.numpy as jnp
from jax import lax
from jax.experimental import pallas as pl
from jax.experimental.pallas import tpu as pltpu
from jax.sharding import Mesh, PartitionSpec as P


RIDGE = 0.5
NX, NZ, NY, NC = 4, 2, 8, 2
ROWS, COLS, CH, IMAGES = 16, 8, 512, 128
F32, BF16 = jnp.float32, jnp.bfloat16
AXES = ("x", "z", "y", "c")
NT = (((1,), (1,)), ((), ()))


def vmem_call(body, out_shape, scratch):
    return pl.pallas_call(
        body,
        out_shape=out_shape,
        scratch_shapes=scratch,
        compiler_params=pltpu.CompilerParams(vmem_limit_bytes=48 * 1024 * 1024),
    )


def interleave_body(own_ref, partner_ref, out_ref, rows_ref):
    for t in range(4):
        lanes = slice(t * 128, (t + 1) * 128)
        for j in range(4):
            rows_ref[t, pl.ds(j, IMAGES, stride=8), :] = own_ref[j, :, lanes].astype(F32)
            rows_ref[t, pl.ds(4 + j, IMAGES, stride=8), :] = partner_ref[j, :, lanes].astype(F32)
        out_ref[:, lanes] = rows_ref[t].astype(BF16)


def conv_body(weight_ref, x_ref, out_ref, wide_ref, z_ref):
    taps, group = weight_ref.shape[1], weight_ref.shape[0]
    for t in range(taps):
        for g in range(group):
            at = t * 64 + g * 4
            wide_ref[at : at + 4, :] = weight_ref[g, t].astype(F32)
    wide_ref[576:640, :] = jnp.zeros((64, CH), F32)
    z_ref[0] = jnp.zeros((10, 8, 640), F32)
    z_ref[17] = jnp.zeros((10, 8, 640), F32)
    z_ref[:, 0] = jnp.zeros((18, 8, 640), F32)
    z_ref[:, 9] = jnp.zeros((18, 8, 640), F32)
    x = x_ref[...]
    for lo, hi in ((0, 256), (256, 512), (512, 640)):
        part = lax.dot_general(x, wide_ref[lo:hi, :].astype(BF16), NT, preferred_element_type=F32)
        z_ref[1:17, 1:9, :, lo:hi] = part.reshape(ROWS, COLS, 8, hi - lo)
    lane_lo = lax.broadcasted_iota(jnp.int32, (4, 8, 128), 2) < 64
    row_lo = lax.broadcasted_iota(jnp.int32, (4, 8, 128), 1) < 4
    for h in range(ROWS):
        sums = [None, None]
        for t in range(taps):
            a, b, tile = t // 3, t % 3, (t // 2) * 128
            piece = z_ref[h + a, b : b + 8, :, tile : tile + 128]
            sums[t % 2] = piece if sums[t % 2] is None else sums[t % 2] + piece
        total = sums[0] + pltpu.roll(sums[1], 64, 2)
        pairs = total.reshape(4, 2, 8, 128)
        even, odd = pairs[:, 0], pairs[:, 1]
        first = jnp.where(row_lo, even, pltpu.roll(odd, 4, 1))
        second = jnp.where(row_lo, pltpu.roll(even, 4, 1), odd)
        packed = jnp.where(lane_lo, first, pltpu.roll(second, 64, 2))
        out_ref[h * 32 : (h + 1) * 32, :] = packed.reshape(32, 128).astype(BF16)


def split(a):
    high = a.astype(BF16)
    return high, (a - high.astype(F32)).astype(BF16)


def fine_dot(a, b):
    (ah, al), (bh, bl) = a, b
    total = jnp.dot(ah, bl, preferred_element_type=F32)
    total = total + jnp.dot(al, bh, preferred_element_type=F32)
    return total + jnp.dot(ah, bh, preferred_element_type=F32)


def stats_body(got_ref, pick_ref, lanes_ref, out_ref, rows_ref):
    lane_lo = lax.broadcasted_iota(jnp.int32, (IMAGES, 128), 1) < 64
    even_row = lax.broadcasted_iota(jnp.int32, (IMAGES, 128), 0) % 2 == 0
    eye = (
        lax.broadcasted_iota(jnp.int32, (IMAGES, IMAGES), 0)
        == lax.broadcasted_iota(jnp.int32, (IMAGES, IMAGES), 1)
    ).astype(F32)
    centered = []
    gram = None
    for k in range(NX):
        block = got_ref[k * 128 : (k + 1) * 128, :]
        picked = jnp.dot(pick_ref[...], block, preferred_element_type=F32)
        from0, from1 = picked[:IMAGES], picked[IMAGES:]
        same = jnp.where(lane_lo, from0, from1)
        swapped = pltpu.roll(jnp.where(lane_lo, from1, from0), 64, 1)
        mixed = jnp.where(even_row, same, swapped).astype(BF16)
        x = jnp.dot(mixed, lanes_ref[...], preferred_element_type=F32)
        center = jnp.sum(x, axis=0, keepdims=True) / IMAGES
        x = (x - center).astype(BF16)
        centered.append(x)
        part = lax.dot_general(x, x, NT, preferred_element_type=F32)
        gram = part if gram is None else gram + part
    scaled = gram / (IMAGES - 1)
    squares = jnp.sum(scaled * (scaled + (2.0 * RIDGE) * eye))
    frob = jnp.sqrt(squares + RIDGE * RIDGE * CH)
    u = (scaled + RIDGE * eye) / frob
    u_parts = split(u)
    v = fine_dot(u_parts, u_parts)
    high = fine_dot(split(v), split(0.0625 * v - 0.5625 * u))
    lower = (2.25 * eye - 2.4375 * u) + 1.6875 * v + high
    high, low = split(lower / jnp.sqrt(frob))
    for k in range(NX):
        white = jnp.dot(high, centered[k], preferred_element_type=F32)
        white = white + jnp.dot(low, centered[k], preferred_element_type=F32)
        rows_ref[pl.ds(k, IMAGES, stride=4), :] = white
    out_ref[...] = rows_ref[...].astype(BF16)


def smooth_body(white_ref, weight_ref, out_ref, pad_ref, rows_ref):
    pad_ref[...] = jnp.zeros((18, 40, 128), F32)
    pad_ref[1:17, 4:36, :] = white_ref[...].astype(F32).reshape(ROWS, 32, 128)
    total = None
    for t in range(9):
        a, b = t // 3, t % 3
        piece = pad_ref[a : a + ROWS, 4 * b : 4 * b + 32, :] * weight_ref[t][None]
        total = piece if total is None else total + piece
    rows_ref[...] = total.reshape(512, 128)
    for k in range(NX):
        out_ref[:, k * 128 : (k + 1) * 128] = rows_ref[pl.ds(k, 128, stride=4), :].astype(BF16)


def pick_tables():
    picks = np.zeros((NC, IMAGES, 128), np.float32)
    for c in range(NC):
        for n in range(IMAGES):
            xs, zy = n // 32, (n // 2) % 16
            picks[c, n, zy * 8 + c * 4 + xs] = 1.0
    lanes = np.zeros((128, 128), np.float32)
    for c in range(NC):
        for zy in range(16):
            for k in range(4):
                lanes[c * 64 + zy * 4 + k, zy * 8 + c * 4 + k] = 1.0
    return picks.reshape(NC * IMAGES, 128), lanes


PICKS, LANES = pick_tables()


def exchange(value, axes):
    return lax.all_to_all(value, axes, 0, 0, tiled=True)


def shards(backbone, conv_weight, smooth_weight):
    image = backbone.reshape(ROWS * COLS, CH)
    chunk = conv_weight.transpose(0, 1, 3, 2).reshape(9, 4, CH)
    kernels = exchange(
        jnp.broadcast_to(chunk[None], (NZ * NY,) + chunk.shape), ("z", "y")
    )
    own = lax.all_gather(image, "x")
    partner = lax.ppermute(own, "c", [(0, 1), (1, 0)])
    x = vmem_call(
        interleave_body, jax.ShapeDtypeStruct((1024, CH), BF16), [pltpu.VMEM((4, 1024, 128), F32)]
    )(own, partner)
    features = vmem_call(
        conv_body,
        jax.ShapeDtypeStruct((512, 128), BF16),
        [pltpu.VMEM((640, CH), F32), pltpu.VMEM((18, 10, 8, 640), F32)],
    )(kernels, x)
    got = exchange(features.reshape(128, 4, 128), AXES)
    white = vmem_call(
        stats_body, jax.ShapeDtypeStruct((512, 128), BF16), [pltpu.VMEM((512, 128), F32)]
    )(got.reshape(512, 128), jnp.asarray(PICKS, BF16), jnp.asarray(LANES, BF16))
    back = exchange(white.reshape(128, 4, 128), AXES)
    taps = jnp.tile(smooth_weight.reshape(9, 4, 128), (1, 8, 1))
    out = vmem_call(
        smooth_body,
        jax.ShapeDtypeStruct((128, CH), BF16),
        [pltpu.VMEM((18, 40, 128), F32), pltpu.VMEM((512, 128), F32)],
    )(back.reshape(512, 128), taps)
    return out.reshape(1, ROWS, COLS, CH)


def solution(mesh):
    split = Mesh(
        mesh.devices.reshape(NX, NZ, NY, NC, mesh.shape["rep"]), AXES + ("rep",)
    )
    whole = ("rep",) + AXES
    return jax.shard_map(
        shards,
        mesh=split,
        in_specs=(P(whole, None, None, None), P(None, None, None, whole), P(None, None, "rep")),
        out_specs=P(whole, None, None, None),
        check_vma=False,
    )
```

```python
import jax
import jax.numpy as jnp
from jax import lax
from jax.experimental import pallas as pl
from jax.experimental.pallas import tpu as pltpu
from jax.sharding import Mesh, PartitionSpec as P


RIDGE = 0.5
NX, NZ, NY, NC = 4, 2, 8, 2
ROWS, COLS, CH, IMAGES = 16, 8, 512, 128
F32, BF16 = jnp.float32, jnp.bfloat16
AXES = ("x", "z", "y", "c")
NT = (((1,), (1,)), ((), ()))


def vmem_call(body, out_shape, scratch):
    return pl.pallas_call(
        body,
        out_shape=out_shape,
        scratch_shapes=scratch,
        compiler_params=pltpu.CompilerParams(vmem_limit_bytes=48 * 1024 * 1024),
    )


def interleave_body(own_ref, partner_ref, out_ref, rows_ref):
    for t in range(4):
        lanes = slice(t * 128, (t + 1) * 128)
        for j in range(4):
            rows_ref[t, pl.ds(j, IMAGES, stride=8), :] = own_ref[j, :, lanes].astype(F32)
            rows_ref[t, pl.ds(4 + j, IMAGES, stride=8), :] = partner_ref[j, :, lanes].astype(F32)
        out_ref[:, lanes] = rows_ref[t].astype(BF16)


def conv_body(weight_ref, x_ref, out_ref, wide_ref, z_ref):
    taps, group = weight_ref.shape[1], weight_ref.shape[0]
    wide_ref[512:640, :] = jnp.zeros((128, CH), F32)
    for t in range(taps):
        for g in range(group):
            at = (t // 2) * 128 + g * 8 + (t % 2) * 4
            wide_ref[at : at + 4, :] = weight_ref[g, t].astype(F32)
    z_ref[0] = jnp.zeros((10, 8, 640), F32)
    z_ref[17] = jnp.zeros((10, 8, 640), F32)
    z_ref[:, 0] = jnp.zeros((18, 8, 640), F32)
    z_ref[:, 9] = jnp.zeros((18, 8, 640), F32)
    x = x_ref[...]
    for lo, hi in ((0, 256), (256, 512), (512, 640)):
        part = lax.dot_general(x, wide_ref[lo:hi, :].astype(BF16), NT, preferred_element_type=F32)
        z_ref[1:17, 1:9, :, lo:hi] = part.reshape(ROWS, COLS, 8, hi - lo)
    slot0 = lax.broadcasted_iota(jnp.int32, (4, 8, 128), 2) % 8 < 4
    row_lo = lax.broadcasted_iota(jnp.int32, (4, 8, 128), 1) < 4
    for h in range(ROWS):
        sums = [None, None]
        for t in range(taps):
            a, b, tile = t // 3, t % 3, (t // 2) * 128
            piece = z_ref[h + a, b : b + 8, :, tile : tile + 128]
            sums[t % 2] = piece if sums[t % 2] is None else sums[t % 2] + piece
        total = sums[0] + pltpu.roll(sums[1], 124, 2)
        pairs = total.reshape(4, 2, 8, 128)
        even, odd = pairs[:, 0], pairs[:, 1]
        first = jnp.where(row_lo, even, pltpu.roll(odd, 4, 1))
        second = jnp.where(row_lo, pltpu.roll(even, 4, 1), odd)
        packed = jnp.where(slot0, first, pltpu.roll(second, 4, 2))
        out_ref[h * 32 : (h + 1) * 32, :] = packed.reshape(32, 128).astype(BF16)


def split(a):
    high = a.astype(BF16)
    return high, (a - high.astype(F32)).astype(BF16)


def fine_dot(a, b):
    (ah, al), (bh, bl) = a, b
    total = jnp.dot(ah, bl, preferred_element_type=F32)
    total = total + jnp.dot(al, bh, preferred_element_type=F32)
    return total + jnp.dot(ah, bh, preferred_element_type=F32)


def stats_body(got_ref, out_ref, turn_ref, rows_ref):
    tiles = (16, 8, 128)
    slot0 = lax.broadcasted_iota(jnp.int32, tiles, 2) % 8 < 4
    row_lo = lax.broadcasted_iota(jnp.int32, tiles, 1) < 4
    eye = (
        lax.broadcasted_iota(jnp.int32, (IMAGES, IMAGES), 0)
        == lax.broadcasted_iota(jnp.int32, (IMAGES, IMAGES), 1)
    ).astype(F32)
    centered = []
    gram = None
    for k in range(NX):
        v = got_ref[k * 128 : (k + 1) * 128, :].astype(F32).reshape(tiles)
        mixed = jnp.where(slot0, v, pltpu.roll(v, 4, 1))
        turned = jnp.where(slot0, pltpu.roll(mixed, 124, 2), pltpu.roll(mixed, 4, 2))
        x = jnp.where(row_lo, mixed, turned).reshape(IMAGES, 128)
        center = jnp.sum(x, axis=0, keepdims=True) / IMAGES
        x = (x - center).astype(BF16)
        centered.append(x)
        part = lax.dot_general(x, x, NT, preferred_element_type=F32)
        gram = part if gram is None else gram + part
    scaled = gram / (IMAGES - 1)
    ridged = scaled + RIDGE * eye
    parts = split(ridged)
    square = fine_dot(parts, parts)
    squares = jnp.sum(scaled * (scaled + (2.0 * RIDGE) * eye))
    frob = jnp.sqrt(squares + RIDGE * RIDGE * CH)
    inverse = 1.0 / frob
    u = ridged * inverse
    v = square * inverse * inverse
    high = fine_dot(split(v), split(0.0625 * v - 0.5625 * u))
    lower = (2.25 * eye - 2.4375 * u) + 1.6875 * v + high
    high, low = split(lower / jnp.sqrt(frob))
    for k in range(NX):
        white = jnp.dot(high, centered[k], preferred_element_type=F32)
        turn_ref[k] = white + jnp.dot(low, centered[k], preferred_element_type=F32)
        for xs in range(NX):
            rows_ref[pl.ds(xs * 128 + k, 32, stride=4), :] = turn_ref[k, pl.ds(xs, 32, stride=4), :]
    out_ref[...] = rows_ref[...].astype(BF16)


def smooth_body(white_ref, weight_ref, out_ref, pad_ref, rows_ref):
    pad_ref[...] = jnp.zeros((18, 40, 128), F32)
    pad_ref[1:17, 4:36, :] = white_ref[...].astype(F32).reshape(ROWS, 32, 128)
    total = None
    for t in range(9):
        a, b = t // 3, t % 3
        piece = pad_ref[a : a + ROWS, 4 * b : 4 * b + 32, :] * weight_ref[t][None]
        total = piece if total is None else total + piece
    rows_ref[...] = total.reshape(512, 128)
    for k in range(NX):
        out_ref[:, k * 128 : (k + 1) * 128] = rows_ref[pl.ds(k, 128, stride=4), :].astype(BF16)


def exchange(value, axes):
    return lax.all_to_all(value, axes, 0, 0, tiled=True)


def shards(backbone, conv_weight, smooth_weight):
    image = backbone.reshape(ROWS * COLS, CH)
    chunk = conv_weight.transpose(0, 1, 3, 2).reshape(9, 4, CH)
    kernels = exchange(
        jnp.broadcast_to(chunk[None], (NZ * NY,) + chunk.shape), ("z", "y")
    )
    own = lax.all_gather(image, "x")
    partner = lax.ppermute(own, "c", [(0, 1), (1, 0)])
    x = vmem_call(
        interleave_body, jax.ShapeDtypeStruct((1024, CH), BF16), [pltpu.VMEM((4, 1024, 128), F32)]
    )(own, partner)
    features = vmem_call(
        conv_body,
        jax.ShapeDtypeStruct((512, 128), BF16),
        [pltpu.VMEM((640, CH), F32), pltpu.VMEM((18, 10, 8, 640), F32)],
    )(kernels, x)
    taps = jnp.tile(smooth_weight.reshape(9, 4, 128), (1, 8, 1))
    features, taps = lax.optimization_barrier((features, taps))
    got = exchange(features.reshape(128, 4, 128), AXES)
    white = vmem_call(
        stats_body,
        jax.ShapeDtypeStruct((512, 128), BF16),
        [pltpu.VMEM((NX, 128, 128), F32), pltpu.VMEM((512, 128), F32)],
    )(got.reshape(512, 128))
    back = exchange(white.reshape(128, 4, 128), AXES)
    out = vmem_call(
        smooth_body,
        jax.ShapeDtypeStruct((128, CH), BF16),
        [pltpu.VMEM((18, 40, 128), F32), pltpu.VMEM((512, 128), F32)],
    )(back.reshape(512, 128), taps)
    return out.reshape(1, ROWS, COLS, CH)


def solution(mesh):
    split = Mesh(
        mesh.devices.reshape(NX, NZ, NY, NC, mesh.shape["rep"]), AXES + ("rep",)
    )
    whole = ("rep",) + AXES
    return jax.shard_map(
        shards,
        mesh=split,
        in_specs=(P(whole, None, None, None), P(None, None, None, whole), P(None, None, "rep")),
        out_specs=P(whole, None, None, None),
        check_vma=False,
    )
```

```python
import jax
import jax.numpy as jnp
from jax import lax
from jax.experimental import pallas as pl
from jax.experimental.pallas import tpu as pltpu
from jax.sharding import Mesh, PartitionSpec as P


RIDGE = 0.5
NX, NZ, NY, NC = 4, 2, 8, 2
ROWS, COLS, CH, IMAGES = 16, 8, 512, 128
F32, BF16 = jnp.float32, jnp.bfloat16
AXES = ("x", "z", "y", "c")
NT = (((1,), (1,)), ((), ()))


def vmem_call(body, out_shape, scratch):
    return pl.pallas_call(
        body,
        out_shape=out_shape,
        scratch_shapes=scratch,
        compiler_params=pltpu.CompilerParams(vmem_limit_bytes=48 * 1024 * 1024),
    )


def spread_body(chunk_ref, out_ref, sems):
    copies = [
        pltpu.make_async_copy(chunk_ref, out_ref.at[g], sems.at[g]) for g in range(NZ * NY)
    ]
    for copy in copies:
        copy.start()
    for copy in copies:
        copy.wait()


def convolve(image_ref, wide, rows_ref, z_ref, put):
    for t in range(4):
        for j in range(NX):
            rows_ref[t, pl.ds(j, IMAGES, stride=4), :] = image_ref[
                j, :, t * 128 : (t + 1) * 128
            ].astype(F32)
    x = jnp.concatenate([rows_ref[t].astype(BF16) for t in range(4)], axis=1)
    z_ref[:, 0] = jnp.zeros((5, 48, 128), F32)
    z_ref[:, 17] = jnp.zeros((5, 48, 128), F32)
    z_ref[:, :, 0:8] = jnp.zeros((5, 18, 8, 128), F32)
    z_ref[:, :, 40:48] = jnp.zeros((5, 18, 8, 128), F32)
    for lo, hi in ((0, 256), (256, 512), (512, 640)):
        part = lax.dot_general(x, wide(lo, hi), NT, preferred_element_type=F32)
        for at in range(lo, hi, 128):
            z_ref[at // 128, 1:17, 8:40] = part[:, at - lo : at - lo + 128].reshape(ROWS, 32, 128)
    for h in range(ROWS):
        sums = [None, None]
        for t in range(9):
            a, b = t // 3, t % 3
            piece = z_ref[t // 2, h + a, 4 + 4 * b : 36 + 4 * b, :]
            sums[t % 2] = piece if sums[t % 2] is None else sums[t % 2] + piece
        put(h, sums[0] + pltpu.roll(sums[1], 124, 1))


def conv_own_body(weight_ref, image_ref, out_ref, wide_ref, tall_ref, rows_ref, z_ref):
    tall_ref[512:640, :] = jnp.zeros((128, CH), F32)
    for t in range(9):
        for g in range(NZ * NY):
            at = (t // 2) * 128 + g * 8 + (t % 2) * 4
            tall_ref[at : at + 4, :] = weight_ref[g, t].astype(F32)
    wide_ref[...] = tall_ref[...].astype(BF16)

    def put(h, total):
        out_ref[h * 32 : (h + 1) * 32, :] = total.astype(BF16)

    convolve(image_ref, lambda lo, hi: wide_ref[lo:hi, :], rows_ref, z_ref, put)


def conv_partner_body(wide_ref, image_ref, own_ref, out_ref, rows_ref, z_ref):
    slot0 = lax.broadcasted_iota(jnp.int32, (32, 128), 1) % 8 < 4

    def put(h, total):
        own = own_ref[h * 32 : (h + 1) * 32, :].astype(F32)
        merged = jnp.where(slot0, own, pltpu.roll(total, 4, 1))
        out_ref[h * 32 : (h + 1) * 32, :] = merged.astype(BF16)

    convolve(image_ref, lambda lo, hi: wide_ref[lo:hi, :], rows_ref, z_ref, put)


def split(a):
    high = a.astype(BF16)
    return high, (a - high.astype(F32)).astype(BF16)


def fine_dot(a, b):
    (ah, al), (bh, bl) = a, b
    total = jnp.dot(ah, bl, preferred_element_type=F32)
    total = total + jnp.dot(al, bh, preferred_element_type=F32)
    return total + jnp.dot(ah, bh, preferred_element_type=F32)


def stats_body(got_ref, out_ref, turn_ref, rows_ref):
    tiles = (16, 8, 128)
    slot0 = lax.broadcasted_iota(jnp.int32, tiles, 2) % 8 < 4
    row_lo = lax.broadcasted_iota(jnp.int32, tiles, 1) < 4
    eye = (
        lax.broadcasted_iota(jnp.int32, (IMAGES, IMAGES), 0)
        == lax.broadcasted_iota(jnp.int32, (IMAGES, IMAGES), 1)
    ).astype(F32)
    centered = []
    gram = None
    for k in range(NX):
        v = got_ref[k * 128 : (k + 1) * 128, :].astype(F32).reshape(tiles)
        mixed = jnp.where(slot0, v, pltpu.roll(v, 4, 1))
        turned = jnp.where(slot0, pltpu.roll(mixed, 124, 2), pltpu.roll(mixed, 4, 2))
        x = jnp.where(row_lo, mixed, turned).reshape(IMAGES, 128)
        center = jnp.sum(x, axis=0, keepdims=True) / IMAGES
        x = (x - center).astype(BF16)
        centered.append(x)
        part = lax.dot_general(x, x, NT, preferred_element_type=F32)
        gram = part if gram is None else gram + part
    scaled = gram / (IMAGES - 1)
    ridged = scaled + RIDGE * eye
    parts = split(ridged)
    square = fine_dot(parts, parts)
    squares = jnp.sum(scaled * (scaled + (2.0 * RIDGE) * eye))
    frob = jnp.sqrt(squares + RIDGE * RIDGE * CH)
    inverse = 1.0 / frob
    u = ridged * inverse
    v = square * inverse * inverse
    high = fine_dot(split(v), split(0.0625 * v - 0.5625 * u))
    lower = (2.25 * eye - 2.4375 * u) + 1.6875 * v + high
    high, low = split(lower / jnp.sqrt(frob))
    for k in range(NX):
        white = jnp.dot(high, centered[k], preferred_element_type=F32)
        turn_ref[k] = white + jnp.dot(low, centered[k], preferred_element_type=F32)
        for xs in range(NX):
            rows_ref[pl.ds(xs * 128 + k, 32, stride=4), :] = turn_ref[k, pl.ds(xs, 32, stride=4), :]
    out_ref[...] = rows_ref[...].astype(BF16)


def smooth_body(white_ref, weight_ref, out_ref, pad_ref, rows_ref):
    pad_ref[0] = jnp.zeros((48, 128), F32)
    pad_ref[17] = jnp.zeros((48, 128), F32)
    pad_ref[:, 0:8] = jnp.zeros((18, 8, 128), F32)
    pad_ref[:, 40:48] = jnp.zeros((18, 8, 128), F32)
    pad_ref[1:17, 8:40, :] = white_ref[...].astype(F32).reshape(ROWS, 32, 128)
    for h in range(ROWS):
        total = None
        for t in range(9):
            a, b = t // 3, t % 3
            piece = pad_ref[h + a, 4 + 4 * b : 36 + 4 * b, :].reshape(4, 8, 128) * weight_ref[t]
            total = piece if total is None else total + piece
        rows_ref[h * 32 : (h + 1) * 32, :] = total.reshape(32, 128)
    for k in range(NX):
        out_ref[:, k * 128 : (k + 1) * 128] = rows_ref[pl.ds(k, 128, stride=4), :].astype(BF16)


def exchange(value, axes):
    return lax.all_to_all(value, axes, 0, 0, tiled=True)


def shards(backbone, conv_weight, smooth_weight):
    image = backbone.reshape(ROWS * COLS, CH)
    chunk = conv_weight.transpose(0, 1, 3, 2).reshape(9, 4, CH)
    spread = pl.pallas_call(
        spread_body,
        out_shape=jax.ShapeDtypeStruct((NZ * NY,) + chunk.shape, BF16),
        in_specs=[pl.BlockSpec(memory_space=pl.ANY)],
        out_specs=pl.BlockSpec(memory_space=pl.ANY),
        scratch_shapes=[pltpu.SemaphoreType.DMA((NZ * NY,))],
        name="spread",
    )(chunk)
    kernels = exchange(spread, ("z", "y"))
    own = lax.all_gather(image, "x")
    partner = lax.ppermute(own, "c", [(0, 1), (1, 0)])
    rows = [pltpu.VMEM((4, 512, 128), F32), pltpu.VMEM((5, 18, 48, 128), F32)]
    half = jax.ShapeDtypeStruct((512, 128), BF16)
    first, wide = vmem_call(
        conv_own_body,
        (half, jax.ShapeDtypeStruct((640, CH), BF16)),
        [pltpu.VMEM((640, CH), F32)] + rows,
    )(kernels, own)
    features = vmem_call(conv_partner_body, half, rows)(wide, partner, first)
    taps = jnp.tile(smooth_weight.reshape(9, 4, 128), (1, 2, 1))
    features, taps = lax.optimization_barrier((features, taps))
    got = exchange(features.reshape(128, 4, 128), AXES)
    white = vmem_call(
        stats_body,
        jax.ShapeDtypeStruct((512, 128), BF16),
        [pltpu.VMEM((NX, 128, 128), F32), pltpu.VMEM((512, 128), F32)],
    )(got.reshape(512, 128))
    back = exchange(white.reshape(128, 4, 128), AXES)
    out = vmem_call(
        smooth_body,
        jax.ShapeDtypeStruct((128, CH), BF16),
        [pltpu.VMEM((18, 48, 128), F32), pltpu.VMEM((512, 128), F32)],
    )(back.reshape(512, 128), taps)
    return out.reshape(1, ROWS, COLS, CH)


def solution(mesh):
    split = Mesh(
        mesh.devices.reshape(NX, NZ, NY, NC, mesh.shape["rep"]), AXES + ("rep",)
    )
    whole = ("rep",) + AXES
    return jax.shard_map(
        shards,
        mesh=split,
        in_specs=(P(whole, None, None, None), P(None, None, None, whole), P(None, None, "rep")),
        out_specs=P(whole, None, None, None),
        check_vma=False,
    )
```

```python
import jax
import jax.numpy as jnp
from jax import lax
from jax.experimental import pallas as pl
from jax.experimental.pallas import tpu as pltpu
from jax.sharding import Mesh, PartitionSpec as P


RIDGE = 0.5
NX, NZ, NY, NC = 4, 2, 8, 2
ROWS, COLS, CH, IMAGES = 16, 8, 512, 128
F32, BF16 = jnp.float32, jnp.bfloat16
AXES = ("x", "z", "y", "c")
NT = (((1,), (1,)), ((), ()))


def vmem_call(body, out_shape, scratch):
    return pl.pallas_call(
        body,
        out_shape=out_shape,
        scratch_shapes=scratch,
        compiler_params=pltpu.CompilerParams(vmem_limit_bytes=48 * 1024 * 1024),
    )


def convolve(image_ref, wide, rows_ref, z_ref, put):
    for t in range(4):
        for j in range(NX):
            rows_ref[t, pl.ds(j, IMAGES, stride=4), :] = image_ref[
                j, :, t * 128 : (t + 1) * 128
            ].astype(F32)
    x = jnp.concatenate([rows_ref[t].astype(BF16) for t in range(4)], axis=1)
    z_ref[:, 0] = jnp.zeros((5, 48, 128), F32)
    z_ref[:, 17] = jnp.zeros((5, 48, 128), F32)
    z_ref[:, :, 0:8] = jnp.zeros((5, 18, 8, 128), F32)
    z_ref[:, :, 40:48] = jnp.zeros((5, 18, 8, 128), F32)
    for lo, hi in ((0, 256), (256, 512), (512, 640)):
        part = lax.dot_general(x, wide(lo, hi), NT, preferred_element_type=F32)
        for at in range(lo, hi, 128):
            z_ref[at // 128, 1:17, 8:40] = part[:, at - lo : at - lo + 128].reshape(ROWS, 32, 128)
    for h in range(ROWS):
        sums = [None, None]
        for t in range(9):
            a, b = t // 3, t % 3
            piece = z_ref[t // 2, h + a, 4 + 4 * b : 36 + 4 * b, :]
            sums[t % 2] = piece if sums[t % 2] is None else sums[t % 2] + piece
        put(h, sums[0] + pltpu.roll(sums[1], 124, 1))


def conv_own_body(weight_ref, image_ref, out_ref, wide_ref, tall_ref, rows_ref, z_ref):
    tall_ref[512:640, :] = jnp.zeros((128, CH), F32)
    for t in range(9):
        for g in range(NZ * NY):
            at = (t // 2) * 128 + g * 8 + (t % 2) * 4
            tall_ref[at : at + 4, :] = weight_ref[g, t].astype(F32)
    wide_ref[...] = tall_ref[...].astype(BF16)

    def put(h, total):
        out_ref[h * 32 : (h + 1) * 32, :] = total.astype(BF16)

    convolve(image_ref, lambda lo, hi: wide_ref[lo:hi, :], rows_ref, z_ref, put)


def conv_partner_body(wide_ref, image_ref, own_ref, out_ref, rows_ref, z_ref):
    slot0 = lax.broadcasted_iota(jnp.int32, (32, 128), 1) % 8 < 4

    def put(h, total):
        own = own_ref[h * 32 : (h + 1) * 32, :].astype(F32)
        merged = jnp.where(slot0, own, pltpu.roll(total, 4, 1))
        out_ref[h * 32 : (h + 1) * 32, :] = merged.astype(BF16)

    convolve(image_ref, lambda lo, hi: wide_ref[lo:hi, :], rows_ref, z_ref, put)


def split(a):
    high = a.astype(BF16)
    return high, (a - high.astype(F32)).astype(BF16)


def fine_dot(a, b):
    (ah, al), (bh, bl) = a, b
    total = jnp.dot(ah, bl, preferred_element_type=F32)
    total = total + jnp.dot(al, bh, preferred_element_type=F32)
    return total + jnp.dot(ah, bh, preferred_element_type=F32)


def stats_body(got_ref, out_ref, turn_ref, rows_ref):
    tiles = (16, 8, 128)
    slot0 = lax.broadcasted_iota(jnp.int32, tiles, 2) % 8 < 4
    row_lo = lax.broadcasted_iota(jnp.int32, tiles, 1) < 4
    eye = (
        lax.broadcasted_iota(jnp.int32, (IMAGES, IMAGES), 0)
        == lax.broadcasted_iota(jnp.int32, (IMAGES, IMAGES), 1)
    ).astype(F32)
    centered = []
    gram = None
    for k in range(NX):
        v = got_ref[k * 128 : (k + 1) * 128, :].astype(F32).reshape(tiles)
        mixed = jnp.where(slot0, v, pltpu.roll(v, 4, 1))
        turned = jnp.where(slot0, pltpu.roll(mixed, 124, 2), pltpu.roll(mixed, 4, 2))
        x = jnp.where(row_lo, mixed, turned).reshape(IMAGES, 128)
        center = jnp.sum(x, axis=0, keepdims=True) / IMAGES
        x = (x - center).astype(BF16)
        centered.append(x)
        part = lax.dot_general(x, x, NT, preferred_element_type=F32)
        gram = part if gram is None else gram + part
    scaled = gram / (IMAGES - 1)
    ridged = scaled + RIDGE * eye
    parts = split(ridged)
    square = fine_dot(parts, parts)
    squares = jnp.sum(scaled * (scaled + (2.0 * RIDGE) * eye))
    frob = jnp.sqrt(squares + RIDGE * RIDGE * CH)
    inverse = 1.0 / frob
    u = ridged * inverse
    v = square * inverse * inverse
    high = fine_dot(split(v), split(0.0625 * v - 0.5625 * u))
    lower = (2.25 * eye - 2.4375 * u) + 1.6875 * v + high
    high, low = split(lower / jnp.sqrt(frob))
    for k in range(NX):
        white = jnp.dot(high, centered[k], preferred_element_type=F32)
        turn_ref[k] = white + jnp.dot(low, centered[k], preferred_element_type=F32)
        for xs in range(NX):
            rows_ref[pl.ds(xs * 128 + k, 32, stride=4), :] = turn_ref[k, pl.ds(xs, 32, stride=4), :]
    out_ref[...] = rows_ref[...].astype(BF16)


def smooth_body(white_ref, weight_ref, out_ref, pad_ref, rows_ref):
    pad_ref[0] = jnp.zeros((48, 128), F32)
    pad_ref[17] = jnp.zeros((48, 128), F32)
    pad_ref[:, 0:8] = jnp.zeros((18, 8, 128), F32)
    pad_ref[:, 40:48] = jnp.zeros((18, 8, 128), F32)
    pad_ref[1:17, 8:40, :] = white_ref[...].astype(F32).reshape(ROWS, 32, 128)
    for h in range(ROWS):
        total = None
        for t in range(9):
            a, b = t // 3, t % 3
            piece = pad_ref[h + a, 4 + 4 * b : 36 + 4 * b, :].reshape(4, 8, 128) * weight_ref[t]
            total = piece if total is None else total + piece
        rows_ref[h * 32 : (h + 1) * 32, :] = total.reshape(32, 128)
    for k in range(NX):
        out_ref[:, k * 128 : (k + 1) * 128] = rows_ref[pl.ds(k, 128, stride=4), :].astype(BF16)


def exchange(value, axes):
    return lax.all_to_all(value, axes, 0, 0, tiled=True)


def shards(backbone, conv_weight, smooth_weight):
    image = backbone.reshape(ROWS * COLS, CH)
    chunk = conv_weight.transpose(0, 1, 3, 2).reshape(9, 4, CH)
    kernels = exchange(
        jnp.broadcast_to(chunk[None], (NZ * NY,) + chunk.shape), ("z", "y")
    )
    own = lax.all_gather(image, "x")
    partner = lax.ppermute(own, "c", [(0, 1), (1, 0)])
    rows = [pltpu.VMEM((4, 512, 128), F32), pltpu.VMEM((5, 18, 48, 128), F32)]
    half = jax.ShapeDtypeStruct((512, 128), BF16)
    first, wide = vmem_call(
        conv_own_body,
        (half, jax.ShapeDtypeStruct((640, CH), BF16)),
        [pltpu.VMEM((640, CH), F32)] + rows,
    )(kernels, own)
    features = vmem_call(conv_partner_body, half, rows)(wide, partner, first)
    taps = jnp.tile(smooth_weight.reshape(9, 4, 128), (1, 2, 1))
    features, taps = lax.optimization_barrier((features, taps))
    got = exchange(features.reshape(128, 4, 128), AXES)
    white = vmem_call(
        stats_body,
        jax.ShapeDtypeStruct((512, 128), BF16),
        [pltpu.VMEM((NX, 128, 128), F32), pltpu.VMEM((512, 128), F32)],
    )(got.reshape(512, 128))
    back = exchange(white.reshape(128, 4, 128), AXES)
    out = vmem_call(
        smooth_body,
        jax.ShapeDtypeStruct((128, CH), BF16),
        [pltpu.VMEM((18, 48, 128), F32), pltpu.VMEM((512, 128), F32)],
    )(back.reshape(512, 128), taps)
    return out.reshape(1, ROWS, COLS, CH)


def solution(mesh):
    split = Mesh(
        mesh.devices.reshape(NX, NZ, NY, NC, mesh.shape["rep"]), AXES + ("rep",)
    )
    whole = ("rep",) + AXES
    return jax.shard_map(
        shards,
        mesh=split,
        in_specs=(P(whole, None, None, None), P(None, None, None, whole), P(None, None, "rep")),
        out_specs=P(whole, None, None, None),
        check_vma=False,
    )
```

```python
import jax
import jax.numpy as jnp
from jax import lax
from jax.experimental import pallas as pl
from jax.experimental.pallas import tpu as pltpu
from jax.sharding import Mesh, PartitionSpec as P


RIDGE = 0.5
NX, NZ, NY, NC = 4, 2, 8, 2
ROWS, COLS, CH, IMAGES = 16, 8, 512, 128
F32, BF16 = jnp.float32, jnp.bfloat16
AXES = ("x", "z", "y", "c")
NT = (((1,), (1,)), ((), ()))


def vmem_call(body, out_shape, scratch):
    return pl.pallas_call(
        body,
        out_shape=out_shape,
        scratch_shapes=scratch,
        compiler_params=pltpu.CompilerParams(vmem_limit_bytes=48 * 1024 * 1024),
    )


def convolve(image_ref, wide, rows_ref, z_ref, put):
    for t in range(4):
        for j in range(NX):
            rows_ref[t, pl.ds(j, IMAGES, stride=4), :] = image_ref[
                j, :, t * 128 : (t + 1) * 128
            ].astype(F32)
    x = jnp.concatenate([rows_ref[t].astype(BF16) for t in range(4)], axis=1)
    z_ref[:, 0] = jnp.zeros((5, 48, 128), F32)
    z_ref[:, 17] = jnp.zeros((5, 48, 128), F32)
    z_ref[:, :, 0:8] = jnp.zeros((5, 18, 8, 128), F32)
    z_ref[:, :, 40:48] = jnp.zeros((5, 18, 8, 128), F32)
    for lo, hi in ((0, 256), (256, 512), (512, 640)):
        part = lax.dot_general(x, wide(lo, hi), NT, preferred_element_type=F32)
        for at in range(lo, hi, 128):
            z_ref[at // 128, 1:17, 8:40] = part[:, at - lo : at - lo + 128].reshape(ROWS, 32, 128)
    for h in range(ROWS):
        sums = [None, None]
        for t in range(9):
            a, b = t // 3, t % 3
            piece = z_ref[t // 2, h + a, 4 + 4 * b : 36 + 4 * b, :]
            sums[t % 2] = piece if sums[t % 2] is None else sums[t % 2] + piece
        put(h, sums[0] + pltpu.roll(sums[1], 124, 1))


def conv_own_body(weight_ref, image_ref, out_ref, wide_ref, tall_ref, rows_ref, z_ref):
    tall_ref[512:640, :] = jnp.zeros((128, CH), F32)
    for t in range(9):
        for g in range(NZ * NY):
            at = (t // 2) * 128 + g * 8 + (t % 2) * 4
            tall_ref[at : at + 4, :] = weight_ref[g, t].astype(F32)
    wide_ref[...] = tall_ref[...].astype(BF16)

    def put(h, total):
        out_ref[h * 32 : (h + 1) * 32, :] = total.astype(BF16)

    convolve(image_ref, lambda lo, hi: wide_ref[lo:hi, :], rows_ref, z_ref, put)


def conv_partner_body(wide_ref, image_ref, own_ref, out_ref, rows_ref, z_ref):
    slot0 = lax.broadcasted_iota(jnp.int32, (32, 128), 1) % 8 < 4

    def put(h, total):
        own = own_ref[h * 32 : (h + 1) * 32, :].astype(F32)
        merged = jnp.where(slot0, own, pltpu.roll(total, 4, 1))
        out_ref[h * 32 : (h + 1) * 32, :] = merged.astype(BF16)

    convolve(image_ref, lambda lo, hi: wide_ref[lo:hi, :], rows_ref, z_ref, put)


def split(a):
    high = a.astype(BF16)
    return high, (a - high.astype(F32)).astype(BF16)


def fine_dot(a, b):
    (ah, al), (bh, bl) = a, b
    total = jnp.dot(ah, bl, preferred_element_type=F32)
    total = total + jnp.dot(al, bh, preferred_element_type=F32)
    return total + jnp.dot(ah, bh, preferred_element_type=F32)


def stats_body(got_ref, out_ref, turn_ref, rows_ref):
    tiles = (16, 8, 128)
    slot0 = lax.broadcasted_iota(jnp.int32, tiles, 2) % 8 < 4
    row_lo = lax.broadcasted_iota(jnp.int32, tiles, 1) < 4
    eye = (
        lax.broadcasted_iota(jnp.int32, (IMAGES, IMAGES), 0)
        == lax.broadcasted_iota(jnp.int32, (IMAGES, IMAGES), 1)
    ).astype(F32)
    centered = []
    gram = None
    for k in range(NX):
        v = got_ref[k * 128 : (k + 1) * 128, :].astype(F32).reshape(tiles)
        mixed = jnp.where(slot0, v, pltpu.roll(v, 4, 1))
        turned = jnp.where(slot0, pltpu.roll(mixed, 124, 2), pltpu.roll(mixed, 4, 2))
        x = jnp.where(row_lo, mixed, turned).reshape(IMAGES, 128)
        center = jnp.sum(x, axis=0, keepdims=True) / IMAGES
        x = (x - center).astype(BF16)
        centered.append(x)
        part = lax.dot_general(x, x, NT, preferred_element_type=F32)
        gram = part if gram is None else gram + part
    scaled = gram / (IMAGES - 1)
    ridged = scaled + RIDGE * eye
    parts = split(ridged)
    square = fine_dot(parts, parts)
    squares = jnp.sum(scaled * (scaled + (2.0 * RIDGE) * eye))
    frob = jnp.sqrt(squares + RIDGE * RIDGE * CH)
    inverse = 1.0 / frob
    u = ridged * inverse
    v = square * inverse * inverse
    high = fine_dot(split(v), split(0.0625 * v - 0.5625 * u))
    lower = (2.25 * eye - 2.4375 * u) + 1.6875 * v + high
    high, low = split(lower / jnp.sqrt(frob))
    for k in range(NX):
        white = jnp.dot(high, centered[k], preferred_element_type=F32)
        turn_ref[k] = white + jnp.dot(low, centered[k], preferred_element_type=F32)
        for c in range(NC):
            for r in range(NX):
                xs = NX - 1 - r if c else r
                rows_ref[pl.ds(xs * 128 + c * 4 + k, 16, stride=8), :] = turn_ref[
                    k, pl.ds(c * 4 + r, 16, stride=8), :
                ]
    out_ref[...] = rows_ref[...].astype(BF16)


def smooth_body(white_ref, weight_ref, out_ref, pad_ref, rows_ref):
    pad_ref[0] = jnp.zeros((48, 128), F32)
    pad_ref[17] = jnp.zeros((48, 128), F32)
    pad_ref[:, 0:8] = jnp.zeros((18, 8, 128), F32)
    pad_ref[:, 40:48] = jnp.zeros((18, 8, 128), F32)
    pad_ref[1:17, 8:40, :] = white_ref[...].astype(F32).reshape(ROWS, 32, 128)
    for h in range(ROWS):
        total = None
        for t in range(9):
            a, b = t // 3, t % 3
            piece = pad_ref[h + a, 4 + 4 * b : 36 + 4 * b, :].reshape(4, 8, 128) * weight_ref[t]
            total = piece if total is None else total + piece
        rows_ref[h * 32 : (h + 1) * 32, :] = total.reshape(32, 128)
    for k in range(NX):
        out_ref[:, k * 128 : (k + 1) * 128] = rows_ref[pl.ds(k, 128, stride=4), :].astype(BF16)


def exchange(value, axes):
    return lax.all_to_all(value, axes, 0, 0, tiled=True)


def shards(backbone, conv_weight, smooth_weight):
    image = backbone.reshape(ROWS * COLS, CH)
    chunk = conv_weight.transpose(0, 1, 3, 2).reshape(9, 4, CH)
    kernels = exchange(
        jnp.broadcast_to(chunk[None], (NZ * NY,) + chunk.shape), ("z", "y")
    )
    ways = [[2 * i for i in range(NX)], [2 * i + 1 for i in reversed(range(NX))]]
    own = lax.all_gather(image, ("x", "c"), axis_index_groups=ways)
    partner = lax.ppermute(own, "c", [(0, 1), (1, 0)])
    rows = [pltpu.VMEM((4, 512, 128), F32), pltpu.VMEM((5, 18, 48, 128), F32)]
    half = jax.ShapeDtypeStruct((512, 128), BF16)
    first, wide = vmem_call(
        conv_own_body,
        (half, jax.ShapeDtypeStruct((640, CH), BF16)),
        [pltpu.VMEM((640, CH), F32)] + rows,
    )(kernels, own)
    features = vmem_call(conv_partner_body, half, rows)(wide, partner, first)
    taps = jnp.tile(smooth_weight.reshape(9, 4, 128), (1, 2, 1))
    features, taps = lax.optimization_barrier((features, taps))
    got = exchange(features.reshape(128, 4, 128), AXES)
    white = vmem_call(
        stats_body,
        jax.ShapeDtypeStruct((512, 128), BF16),
        [pltpu.VMEM((NX, 128, 128), F32), pltpu.VMEM((512, 128), F32)],
    )(got.reshape(512, 128))
    back = exchange(white.reshape(128, 4, 128), AXES)
    out = vmem_call(
        smooth_body,
        jax.ShapeDtypeStruct((128, CH), BF16),
        [pltpu.VMEM((18, 48, 128), F32), pltpu.VMEM((512, 128), F32)],
    )(back.reshape(512, 128), taps)
    return out.reshape(1, ROWS, COLS, CH)


def solution(mesh):
    split = Mesh(
        mesh.devices.reshape(NX, NZ, NY, NC, mesh.shape["rep"]), AXES + ("rep",)
    )
    whole = ("rep",) + AXES
    return jax.shard_map(
        shards,
        mesh=split,
        in_specs=(P(whole, None, None, None), P(None, None, None, whole), P(None, None, "rep")),
        out_specs=P(whole, None, None, None),
        check_vma=False,
    )
```

```python
import jax
import jax.numpy as jnp
from jax import lax
from jax.experimental import pallas as pl
from jax.experimental.pallas import tpu as pltpu
from jax.sharding import Mesh, PartitionSpec as P


RIDGE = 0.5
NX, NZ, NY, NC = 4, 2, 8, 2
ROWS, COLS, CH, IMAGES = 16, 8, 512, 128
F32, BF16 = jnp.float32, jnp.bfloat16
AXES = ("x", "z", "y", "c")
NT = (((1,), (1,)), ((), ()))


def vmem_call(body, out_shape, scratch):
    return pl.pallas_call(
        body,
        out_shape=out_shape,
        scratch_shapes=scratch,
        compiler_params=pltpu.CompilerParams(vmem_limit_bytes=48 * 1024 * 1024),
    )


def convolve(image_ref, half, wide, rows_ref, z_ref, put):
    for t in range(4):
        for j in range(NX):
            rows_ref[t, pl.ds(j, IMAGES, stride=4), :] = image_ref[
                NZ * j + half, :, t * 128 : (t + 1) * 128
            ].astype(F32)
    x = jnp.concatenate([rows_ref[t].astype(BF16) for t in range(4)], axis=1)
    z_ref[:, 0] = jnp.zeros((5, 48, 128), F32)
    z_ref[:, 17] = jnp.zeros((5, 48, 128), F32)
    z_ref[:, :, 0:8] = jnp.zeros((5, 18, 8, 128), F32)
    z_ref[:, :, 40:48] = jnp.zeros((5, 18, 8, 128), F32)
    for lo, hi in ((0, 256), (256, 512), (512, 640)):
        part = lax.dot_general(x, wide(lo, hi), NT, preferred_element_type=F32)
        for at in range(lo, hi, 128):
            z_ref[at // 128, 1:17, 8:40] = part[:, at - lo : at - lo + 128].reshape(ROWS, 32, 128)
    for h in range(ROWS):
        sums = [None, None]
        for t in range(9):
            a, b = t // 3, t % 3
            piece = z_ref[t // 2, h + a, 4 + 4 * b : 36 + 4 * b, :]
            sums[t % 2] = piece if sums[t % 2] is None else sums[t % 2] + piece
        put(h, sums[0] + pltpu.roll(sums[1], 64, 1))


def conv_first_body(weight_ref, image_ref, out_ref, wide_ref, tall_ref, rows_ref, z_ref):
    tall_ref[576:640, :] = jnp.zeros((64, CH), F32)
    for t in range(9):
        for g in range(NY * NC):
            at = t * 64 + g * 4
            tall_ref[at : at + 4, :] = weight_ref[g, t].astype(F32)
    wide_ref[...] = tall_ref[...].astype(BF16)

    def put(h, total):
        out_ref[h * 32 : (h + 1) * 32, :] = total.astype(BF16)

    convolve(image_ref, 0, lambda lo, hi: wide_ref[lo:hi, :], rows_ref, z_ref, put)


def conv_second_body(wide_ref, image_ref, own_ref, out_ref, rows_ref, z_ref):
    lane_lo = lax.broadcasted_iota(jnp.int32, (32, 128), 1) < 64

    def put(h, total):
        own = own_ref[h * 32 : (h + 1) * 32, :].astype(F32)
        merged = jnp.where(lane_lo, own, pltpu.roll(total, 64, 1))
        out_ref[h * 32 : (h + 1) * 32, :] = merged.astype(BF16)

    convolve(image_ref, 1, lambda lo, hi: wide_ref[lo:hi, :], rows_ref, z_ref, put)


def split(a):
    high = a.astype(BF16)
    return high, (a - high.astype(F32)).astype(BF16)


def fine_dot(a, b):
    (ah, al), (bh, bl) = a, b
    total = jnp.dot(ah, bl, preferred_element_type=F32)
    total = total + jnp.dot(al, bh, preferred_element_type=F32)
    return total + jnp.dot(ah, bh, preferred_element_type=F32)


def stats_body(got_ref, out_ref, turn_ref, rows_ref):
    lane_lo = lax.broadcasted_iota(jnp.int32, (64, 128), 1) < 64
    eye = (
        lax.broadcasted_iota(jnp.int32, (IMAGES, IMAGES), 0)
        == lax.broadcasted_iota(jnp.int32, (IMAGES, IMAGES), 1)
    ).astype(F32)
    centered = []
    gram = None
    for k in range(NX):
        z0 = got_ref[k * 128 : k * 128 + 64, :].astype(F32)
        z1 = got_ref[k * 128 + 64 : (k + 1) * 128, :].astype(F32)
        even = jnp.where(lane_lo, z0, pltpu.roll(z1, 64, 1))
        odd = jnp.where(lane_lo, pltpu.roll(z0, 64, 1), z1)
        x = jnp.concatenate([even, odd], axis=0)
        center = jnp.sum(x, axis=0, keepdims=True) / IMAGES
        x = (x - center).astype(BF16)
        centered.append(x)
        part = lax.dot_general(x, x, NT, preferred_element_type=F32)
        gram = part if gram is None else gram + part
    scaled = gram / (IMAGES - 1)
    ridged = scaled + RIDGE * eye
    parts = split(ridged)
    square = fine_dot(parts, parts)
    squares = jnp.sum(scaled * (scaled + (2.0 * RIDGE) * eye))
    frob = jnp.sqrt(squares + RIDGE * RIDGE * CH)
    inverse = 1.0 / frob
    u = ridged * inverse
    v = square * inverse * inverse
    high = fine_dot(split(v), split(0.0625 * v - 0.5625 * u))
    lower = (2.25 * eye - 2.4375 * u) + 1.6875 * v + high
    high, low = split(lower / jnp.sqrt(frob))
    for k in range(NX):
        white = jnp.dot(high, centered[k], preferred_element_type=F32)
        turn_ref[k] = white + jnp.dot(low, centered[k], preferred_element_type=F32)
        for xs in range(NX):
            rows_ref[pl.ds(xs * 128 + k, 32, stride=4), :] = turn_ref[k, pl.ds(xs, 32, stride=4), :]
    out_ref[...] = rows_ref[...].astype(BF16)


def smooth_body(white_ref, weight_ref, out_ref, pad_ref, rows_ref):
    pad_ref[0] = jnp.zeros((48, 128), F32)
    pad_ref[17] = jnp.zeros((48, 128), F32)
    pad_ref[:, 0:8] = jnp.zeros((18, 8, 128), F32)
    pad_ref[:, 40:48] = jnp.zeros((18, 8, 128), F32)
    pad_ref[1:17, 8:40, :] = white_ref[...].astype(F32).reshape(ROWS, 32, 128)
    for h in range(ROWS):
        total = None
        for t in range(9):
            a, b = t // 3, t % 3
            piece = pad_ref[h + a, 4 + 4 * b : 36 + 4 * b, :].reshape(4, 8, 128) * weight_ref[t]
            total = piece if total is None else total + piece
        rows_ref[h * 32 : (h + 1) * 32, :] = total.reshape(32, 128)
    for k in range(NX):
        out_ref[:, k * 128 : (k + 1) * 128] = rows_ref[pl.ds(k, 128, stride=4), :].astype(BF16)


def exchange(value, axes):
    return lax.all_to_all(value, axes, 0, 0, tiled=True)


def shards(backbone, conv_weight, smooth_weight):
    image = backbone.reshape(ROWS * COLS, CH)
    chunk = conv_weight.transpose(0, 1, 3, 2).reshape(9, 4, CH)
    images = exchange(jnp.broadcast_to(image[None], (NX * NZ,) + image.shape), ("x", "z"))
    kernels = lax.all_gather(chunk, ("y", "c"))
    rows = [pltpu.VMEM((4, 512, 128), F32), pltpu.VMEM((5, 18, 48, 128), F32)]
    half = jax.ShapeDtypeStruct((512, 128), BF16)
    first, wide = vmem_call(
        conv_first_body,
        (half, jax.ShapeDtypeStruct((640, CH), BF16)),
        [pltpu.VMEM((640, CH), F32)] + rows,
    )(kernels, images)
    features = vmem_call(conv_second_body, half, rows)(wide, images, first)
    taps = jnp.tile(smooth_weight.reshape(9, 4, 128), (1, 2, 1))
    features, taps = lax.optimization_barrier((features, taps))
    got = exchange(features.reshape(128, 4, 128), AXES)
    white = vmem_call(
        stats_body,
        jax.ShapeDtypeStruct((512, 128), BF16),
        [pltpu.VMEM((NX, 128, 128), F32), pltpu.VMEM((512, 128), F32)],
    )(got.reshape(512, 128))
    back = exchange(white.reshape(128, 4, 128), AXES)
    out = vmem_call(
        smooth_body,
        jax.ShapeDtypeStruct((128, CH), BF16),
        [pltpu.VMEM((18, 48, 128), F32), pltpu.VMEM((512, 128), F32)],
    )(back.reshape(512, 128), taps)
    return out.reshape(1, ROWS, COLS, CH)


def solution(mesh):
    split = Mesh(
        mesh.devices.reshape(NX, NZ, NY, NC, mesh.shape["rep"]), AXES + ("rep",)
    )
    whole = ("rep",) + AXES
    return jax.shard_map(
        shards,
        mesh=split,
        in_specs=(P(whole, None, None, None), P(None, None, None, whole), P(None, None, "rep")),
        out_specs=P(whole, None, None, None),
        check_vma=False,
    )
```

```python
import jax
import jax.numpy as jnp
from jax import lax
from jax.experimental import pallas as pl
from jax.experimental.pallas import tpu as pltpu
from jax.sharding import Mesh, PartitionSpec as P


RIDGE = 0.5
NX, NZ, NY, NC = 4, 2, 8, 2
ROWS, COLS, CH, IMAGES = 16, 8, 512, 128
F32, BF16 = jnp.float32, jnp.bfloat16
AXES = ("x", "z", "y", "c")
NT = (((1,), (1,)), ((), ()))


def vmem_call(body, out_shape, scratch):
    return pl.pallas_call(
        body,
        out_shape=out_shape,
        scratch_shapes=scratch,
        compiler_params=pltpu.CompilerParams(vmem_limit_bytes=48 * 1024 * 1024),
    )


def conv_body(weight_ref, image_ref, out_ref, tall_ref, z_ref, rows_ref):
    tall_ref[576:640, :] = jnp.zeros((64, CH), F32)
    for t in range(9):
        for g in range(NY * NC):
            at = t * 64 + g * 4
            tall_ref[at : at + 4, :] = weight_ref[g, t].astype(F32)
    group = NX * NZ
    z_ref[:, :, 0:16] = jnp.zeros((5, group, 16, 128), F32)
    z_ref[:, :, 144:160] = jnp.zeros((5, group, 16, 128), F32)
    x = image_ref[...].reshape(group * ROWS * COLS, CH)
    for lo, hi in ((0, 256), (256, 512), (512, 640)):
        wide = tall_ref[lo:hi, :].astype(BF16)
        part = lax.dot_general(x, wide, NT, preferred_element_type=F32)
        for at in range(lo, hi, 128):
            z_ref[at // 128, :, 16:144] = part[:, at - lo : at - lo + 128].reshape(group, 128, 128)
    lane_lo = lax.broadcasted_iota(jnp.int32, (32, 128), 1) < 64
    column = lax.broadcasted_iota(jnp.int32, (32, 128), 0) % COLS
    inside = (column > 0, None, column < COLS - 1)
    for j in range(NX):
        for start in range(0, 128, 32):
            halves = []
            for half in range(NZ):
                sums = [0.0, 0.0]
                for b in range(3):
                    parts = [None, None]
                    for a in range(3):
                        t = 3 * a + b
                        at = 16 + start + 8 * (a - 1) + b - 1
                        piece = z_ref[t // 2, NZ * j + half, at : at + 32, :]
                        parts[t % 2] = piece if parts[t % 2] is None else parts[t % 2] + piece
                    for parity in range(2):
                        part = parts[parity]
                        if inside[b] is not None:
                            part = jnp.where(inside[b], part, 0.0)
                        sums[parity] = sums[parity] + part
                halves.append(sums[half] + pltpu.roll(sums[1 - half], 64, 1))
            rows_ref[pl.ds(4 * start + j, 32, stride=4), :] = jnp.where(lane_lo, *halves)
    out_ref[...] = rows_ref[...].astype(BF16)


def split(a):
    high = a.astype(BF16)
    return high, (a - high.astype(F32)).astype(BF16)


def fine_dot(a, b):
    (ah, al), (bh, bl) = a, b
    total = jnp.dot(ah, bl, preferred_element_type=F32)
    total = total + jnp.dot(al, bh, preferred_element_type=F32)
    return total + jnp.dot(ah, bh, preferred_element_type=F32)


def stats_body(got_ref, out_ref, turn_ref, rows_ref):
    lane_lo = lax.broadcasted_iota(jnp.int32, (64, 128), 1) < 64
    eye = (
        lax.broadcasted_iota(jnp.int32, (IMAGES, IMAGES), 0)
        == lax.broadcasted_iota(jnp.int32, (IMAGES, IMAGES), 1)
    ).astype(F32)
    centered = []
    gram = None
    for k in range(NX):
        z0 = got_ref[k * 128 : k * 128 + 64, :].astype(F32)
        z1 = got_ref[k * 128 + 64 : (k + 1) * 128, :].astype(F32)
        even = jnp.where(lane_lo, z0, pltpu.roll(z1, 64, 1))
        odd = jnp.where(lane_lo, pltpu.roll(z0, 64, 1), z1)
        x = jnp.concatenate([even, odd], axis=0)
        center = jnp.sum(x, axis=0, keepdims=True) / IMAGES
        x = (x - center).astype(BF16)
        centered.append(x)
        part = lax.dot_general(x, x, NT, preferred_element_type=F32)
        gram = part if gram is None else gram + part
    scaled = gram / (IMAGES - 1)
    ridged = scaled + RIDGE * eye
    parts = split(ridged)
    square = fine_dot(parts, parts)
    squares = jnp.sum(scaled * (scaled + (2.0 * RIDGE) * eye))
    frob = jnp.sqrt(squares + RIDGE * RIDGE * CH)
    inverse = 1.0 / frob
    u = ridged * inverse
    v = square * inverse * inverse
    high = fine_dot(split(v), split(0.0625 * v - 0.5625 * u))
    lower = (2.25 * eye - 2.4375 * u) + 1.6875 * v + high
    high, low = split(lower / jnp.sqrt(frob))
    for k in range(NX):
        white = jnp.dot(high, centered[k], preferred_element_type=F32)
        turn_ref[k] = white + jnp.dot(low, centered[k], preferred_element_type=F32)
        for xs in range(NX):
            rows_ref[pl.ds(xs * 128 + k, 32, stride=4), :] = turn_ref[k, pl.ds(xs, 32, stride=4), :]
    out_ref[...] = rows_ref[...].astype(BF16)


def smooth_body(white_ref, weight_ref, out_ref, pad_ref, rows_ref):
    pad_ref[0] = jnp.zeros((48, 128), F32)
    pad_ref[17] = jnp.zeros((48, 128), F32)
    pad_ref[:, 0:8] = jnp.zeros((18, 8, 128), F32)
    pad_ref[:, 40:48] = jnp.zeros((18, 8, 128), F32)
    pad_ref[1:17, 8:40, :] = white_ref[...].astype(F32).reshape(ROWS, 32, 128)
    for h in range(ROWS):
        total = None
        for t in range(9):
            a, b = t // 3, t % 3
            piece = pad_ref[h + a, 4 + 4 * b : 36 + 4 * b, :].reshape(4, 8, 128) * weight_ref[t]
            total = piece if total is None else total + piece
        rows_ref[h * 32 : (h + 1) * 32, :] = total.reshape(32, 128)
    for k in range(NX):
        out_ref[:, k * 128 : (k + 1) * 128] = rows_ref[pl.ds(k, 128, stride=4), :].astype(BF16)


def exchange(value, axes):
    return lax.all_to_all(value, axes, 0, 0, tiled=True)


def shards(backbone, conv_weight, smooth_weight):
    image = backbone.reshape(ROWS * COLS, CH)
    chunk = conv_weight.transpose(0, 1, 3, 2).reshape(9, 4, CH)
    group = NX * NZ
    spread = jnp.broadcast_to(image[None], (group,) + image.shape)
    images = exchange(spread, ("x", "z"))
    kernels = lax.all_gather(chunk, ("y", "c"))
    kernels, smooth_weight = lax.optimization_barrier((kernels, smooth_weight))
    taps = jnp.tile(smooth_weight.reshape(9, 4, 128), (1, 2, 1))
    features = vmem_call(
        conv_body,
        jax.ShapeDtypeStruct((512, 128), BF16),
        [
            pltpu.VMEM((640, CH), F32),
            pltpu.VMEM((5, group, 160, 128), F32),
            pltpu.VMEM((512, 128), F32),
        ],
    )(kernels, images)
    features, taps = lax.optimization_barrier((features, taps))
    got = exchange(features.reshape(128, 4, 128), AXES)
    white = vmem_call(
        stats_body,
        jax.ShapeDtypeStruct((512, 128), BF16),
        [pltpu.VMEM((NX, 128, 128), F32), pltpu.VMEM((512, 128), F32)],
    )(got.reshape(512, 128))
    back = exchange(white.reshape(128, 4, 128), AXES)
    out = vmem_call(
        smooth_body,
        jax.ShapeDtypeStruct((128, CH), BF16),
        [pltpu.VMEM((18, 48, 128), F32), pltpu.VMEM((512, 128), F32)],
    )(back.reshape(512, 128), taps)
    return out.reshape(1, ROWS, COLS, CH)


def solution(mesh):
    split = Mesh(
        mesh.devices.reshape(NX, NZ, NY, NC, mesh.shape["rep"]), AXES + ("rep",)
    )
    whole = ("rep",) + AXES
    return jax.shard_map(
        shards,
        mesh=split,
        in_specs=(P(whole, None, None, None), P(None, None, None, whole), P(None, None, "rep")),
        out_specs=P(whole, None, None, None),
        check_vma=False,
    )
```

```python
import jax
import jax.numpy as jnp
from jax import lax
from jax.experimental import pallas as pl
from jax.experimental.pallas import tpu as pltpu
from jax.sharding import Mesh, PartitionSpec as P


RIDGE = 0.5
NX, NZ, NY, NC = 4, 2, 8, 2
ROWS, COLS, CH, IMAGES = 16, 8, 512, 128
F32, BF16 = jnp.float32, jnp.bfloat16
AXES = ("x", "z", "y", "c")
NT = (((1,), (1,)), ((), ()))


def vmem_call(body, out_shape, scratch):
    return pl.pallas_call(
        body,
        out_shape=out_shape,
        scratch_shapes=scratch,
        compiler_params=pltpu.CompilerParams(vmem_limit_bytes=48 * 1024 * 1024),
    )


def conv_body(weight_ref, image_ref, out_ref, tall_ref, z_ref, rows_ref):
    tall_ref[576:640, :] = jnp.zeros((64, CH), F32)
    for t in range(9):
        for g in range(NY * NC):
            at = t * 64 + g * 4
            tall_ref[at : at + 4, :] = weight_ref[g, t].astype(F32)
    group = NX * NZ
    z_ref[:, :, 0:16] = jnp.zeros((5, group, 16, 128), F32)
    z_ref[:, :, 144:160] = jnp.zeros((5, group, 16, 128), F32)
    x = image_ref[...].reshape(group * ROWS * COLS, CH)
    for lo, hi in ((0, 256), (256, 512), (512, 640)):
        wide = tall_ref[lo:hi, :].astype(BF16)
        part = lax.dot_general(x, wide, NT, preferred_element_type=F32)
        for at in range(lo, hi, 128):
            z_ref[at // 128, :, 16:144] = part[:, at - lo : at - lo + 128].reshape(group, 128, 128)
    lane_lo = lax.broadcasted_iota(jnp.int32, (32, 128), 1) < 64
    column = lax.broadcasted_iota(jnp.int32, (32, 128), 0) % COLS
    inside = (column > 0, None, column < COLS - 1)
    for j in range(NX):
        for start in range(0, 128, 32):
            halves = []
            for half in range(NZ):
                sums = [0.0, 0.0]
                for b in range(3):
                    parts = [None, None]
                    for a in range(3):
                        t = 3 * a + b
                        at = 16 + start + 8 * (a - 1) + b - 1
                        piece = z_ref[t // 2, NZ * j + half, at : at + 32, :]
                        parts[t % 2] = piece if parts[t % 2] is None else parts[t % 2] + piece
                    for parity in range(2):
                        part = parts[parity]
                        if inside[b] is not None:
                            part = jnp.where(inside[b], part, 0.0)
                        sums[parity] = sums[parity] + part
                halves.append(sums[half] + pltpu.roll(sums[1 - half], 64, 1))
            rows_ref[pl.ds(4 * start + j, 32, stride=4), :] = jnp.where(lane_lo, *halves)
    out_ref[...] = rows_ref[...].astype(BF16)


def split(a):
    high = a.astype(BF16)
    return high, (a - high.astype(F32)).astype(BF16)


def fine_dot(a, b):
    (ah, al), (bh, bl) = a, b
    total = jnp.dot(ah, bl, preferred_element_type=F32)
    total = total + jnp.dot(al, bh, preferred_element_type=F32)
    return total + jnp.dot(ah, bh, preferred_element_type=F32)


def stats_body(got_ref, out_ref, turn_ref, rows_ref):
    lane_lo = lax.broadcasted_iota(jnp.int32, (64, 128), 1) < 64
    eye = (
        lax.broadcasted_iota(jnp.int32, (IMAGES, IMAGES), 0)
        == lax.broadcasted_iota(jnp.int32, (IMAGES, IMAGES), 1)
    ).astype(F32)
    blocks = []
    for k in range(NX):
        z0 = got_ref[k * 128 : k * 128 + 64, :].astype(F32)
        z1 = got_ref[k * 128 + 64 : (k + 1) * 128, :].astype(F32)
        even = jnp.where(lane_lo, z0, pltpu.roll(z1, 64, 1))
        odd = jnp.where(lane_lo, pltpu.roll(z0, 64, 1), z1)
        x = jnp.concatenate([even, odd], axis=0)
        center = jnp.sum(x, axis=0, keepdims=True) / IMAGES
        blocks.append((x - center).astype(BF16))
    centered = jnp.concatenate(blocks, axis=1)
    gram = lax.dot_general(centered, centered, NT, preferred_element_type=F32)
    scaled = gram / (IMAGES - 1)
    ridged = scaled + RIDGE * eye
    parts = split(ridged)
    square = fine_dot(parts, parts)
    squares = jnp.sum(scaled * (scaled + (2.0 * RIDGE) * eye))
    frob = jnp.sqrt(squares + RIDGE * RIDGE * CH)
    inverse = 1.0 / frob
    u = ridged * inverse
    v = square * inverse * inverse
    high = fine_dot(split(v), split(0.0625 * v - 0.5625 * u))
    lower = (2.25 * eye - 2.4375 * u) + 1.6875 * v + high
    high, low = split(lower / jnp.sqrt(frob))
    white = jnp.dot(high, centered, preferred_element_type=F32)
    white = white + jnp.dot(low, centered, preferred_element_type=F32)
    for k in range(NX):
        turn_ref[k] = white[:, k * 128 : (k + 1) * 128]
        for xs in range(NX):
            rows_ref[pl.ds(xs * 128 + k, 32, stride=4), :] = turn_ref[k, pl.ds(xs, 32, stride=4), :]
    out_ref[...] = rows_ref[...].astype(BF16)


def smooth_body(white_ref, weight_ref, out_ref, pad_ref, rows_ref):
    pad_ref[0] = jnp.zeros((48, 128), F32)
    pad_ref[17] = jnp.zeros((48, 128), F32)
    pad_ref[:, 0:8] = jnp.zeros((18, 8, 128), F32)
    pad_ref[:, 40:48] = jnp.zeros((18, 8, 128), F32)
    pad_ref[1:17, 8:40, :] = white_ref[...].astype(F32).reshape(ROWS, 32, 128)
    for h in range(ROWS):
        total = None
        for t in range(9):
            a, b = t // 3, t % 3
            piece = pad_ref[h + a, 4 + 4 * b : 36 + 4 * b, :].reshape(4, 8, 128) * weight_ref[t]
            total = piece if total is None else total + piece
        rows_ref[h * 32 : (h + 1) * 32, :] = total.reshape(32, 128)
    for k in range(NX):
        out_ref[:, k * 128 : (k + 1) * 128] = rows_ref[pl.ds(k, 128, stride=4), :].astype(BF16)


def exchange(value, axes):
    return lax.all_to_all(value, axes, 0, 0, tiled=True)


def shards(backbone, conv_weight, smooth_weight):
    image = backbone.reshape(ROWS * COLS, CH)
    chunk = conv_weight.transpose(0, 1, 3, 2).reshape(9, 4, CH)
    group = NX * NZ
    spread = jnp.broadcast_to(image[None], (group,) + image.shape)
    images = exchange(spread, ("x", "z"))
    kernels = lax.all_gather(chunk, ("y", "c"))
    kernels, smooth_weight = lax.optimization_barrier((kernels, smooth_weight))
    taps = jnp.tile(smooth_weight.reshape(9, 4, 128), (1, 2, 1))
    features = vmem_call(
        conv_body,
        jax.ShapeDtypeStruct((512, 128), BF16),
        [
            pltpu.VMEM((640, CH), F32),
            pltpu.VMEM((5, group, 160, 128), F32),
            pltpu.VMEM((512, 128), F32),
        ],
    )(kernels, images)
    features, taps = lax.optimization_barrier((features, taps))
    got = exchange(features.reshape(128, 4, 128), AXES)
    white = vmem_call(
        stats_body,
        jax.ShapeDtypeStruct((512, 128), BF16),
        [pltpu.VMEM((NX, 128, 128), F32), pltpu.VMEM((512, 128), F32)],
    )(got.reshape(512, 128))
    back = exchange(white.reshape(128, 4, 128), AXES)
    out = vmem_call(
        smooth_body,
        jax.ShapeDtypeStruct((128, CH), BF16),
        [pltpu.VMEM((18, 48, 128), F32), pltpu.VMEM((512, 128), F32)],
    )(back.reshape(512, 128), taps)
    return out.reshape(1, ROWS, COLS, CH)


def solution(mesh):
    split = Mesh(
        mesh.devices.reshape(NX, NZ, NY, NC, mesh.shape["rep"]), AXES + ("rep",)
    )
    whole = ("rep",) + AXES
    return jax.shard_map(
        shards,
        mesh=split,
        in_specs=(P(whole, None, None, None), P(None, None, None, whole), P(None, None, "rep")),
        out_specs=P(whole, None, None, None),
        check_vma=False,
    )
```

```python
import jax
import jax.numpy as jnp
from jax import lax
from jax.experimental import pallas as pl
from jax.experimental.pallas import tpu as pltpu
from jax.sharding import Mesh, PartitionSpec as P


RIDGE = 0.5
NX, NZ, NY, NC = 4, 2, 8, 2
ROWS, COLS, CH, IMAGES = 16, 8, 512, 128
F32, BF16 = jnp.float32, jnp.bfloat16
AXES = ("x", "z", "y", "c")
NT = (((1,), (1,)), ((), ()))


def vmem_call(body, out_shape, scratch):
    return pl.pallas_call(
        body,
        out_shape=out_shape,
        scratch_shapes=scratch,
        compiler_params=pltpu.CompilerParams(vmem_limit_bytes=48 * 1024 * 1024),
    )


def conv_body(weight_ref, image_ref, out_ref, tall_ref, z_ref, rows_ref):
    group = NX * NZ
    for t in range(9):
        tall_ref[t * 64 : (t + 1) * 64, :] = weight_ref[:, t].astype(F32).reshape(64, CH).astype(BF16)
    tall_ref[576:640, :] = jnp.zeros((64, CH), BF16)
    z_ref[:, :, 0:16] = jnp.zeros((5, group, 16, 128), F32)
    z_ref[:, :, 144:160] = jnp.zeros((5, group, 16, 128), F32)
    x = image_ref[...].reshape(group * ROWS * COLS, CH)
    for lo, hi in ((0, 256), (256, 512), (512, 640)):
        wide = tall_ref[lo:hi, :]
        part = lax.dot_general(x, wide, NT, preferred_element_type=F32)
        for at in range(lo, hi, 128):
            z_ref[at // 128, :, 16:144] = part[:, at - lo : at - lo + 128].reshape(group, 128, 128)
    lane_lo = lax.broadcasted_iota(jnp.int32, (32, 128), 1) < 64
    column = lax.broadcasted_iota(jnp.int32, (32, 128), 0) % COLS
    inside = (column > 0, None, column < COLS - 1)
    for j in range(NX):
        for start in range(0, 128, 32):
            halves = []
            for half in range(NZ):
                sums = [0.0, 0.0]
                for b in range(3):
                    parts = [None, None]
                    for a in range(3):
                        t = 3 * a + b
                        at = 16 + start + 8 * (a - 1) + b - 1
                        piece = z_ref[t // 2, NZ * j + half, at : at + 32, :]
                        parts[t % 2] = piece if parts[t % 2] is None else parts[t % 2] + piece
                    for parity in range(2):
                        part = parts[parity]
                        if inside[b] is not None:
                            part = jnp.where(inside[b], part, 0.0)
                        sums[parity] = sums[parity] + part
                halves.append(sums[half] + pltpu.roll(sums[1 - half], 64, 1))
            rows_ref[pl.ds(4 * start + j, 32, stride=4), :] = jnp.where(lane_lo, *halves)
    out_ref[...] = rows_ref[...].astype(BF16)


def split(a):
    high = a.astype(BF16)
    return high, (a - high.astype(F32)).astype(BF16)


def fine_dot(a, b):
    (ah, al), (bh, bl) = a, b
    total = jnp.dot(ah, bl, preferred_element_type=F32)
    total = total + jnp.dot(al, bh, preferred_element_type=F32)
    return total + jnp.dot(ah, bh, preferred_element_type=F32)


def stats_body(got_ref, out_ref, turn_ref, rows_ref):
    lane_lo = lax.broadcasted_iota(jnp.int32, (64, 128), 1) < 64
    eye = (
        lax.broadcasted_iota(jnp.int32, (IMAGES, IMAGES), 0)
        == lax.broadcasted_iota(jnp.int32, (IMAGES, IMAGES), 1)
    ).astype(F32)
    blocks = []
    for k in range(NX):
        z0 = got_ref[k * 128 : k * 128 + 64, :].astype(F32)
        z1 = got_ref[k * 128 + 64 : (k + 1) * 128, :].astype(F32)
        even = jnp.where(lane_lo, z0, pltpu.roll(z1, 64, 1))
        odd = jnp.where(lane_lo, pltpu.roll(z0, 64, 1), z1)
        x = jnp.concatenate([even, odd], axis=0)
        center = jnp.sum(x, axis=0, keepdims=True) / IMAGES
        blocks.append((x - center).astype(BF16))
    centered = jnp.concatenate(blocks, axis=1)
    gram = lax.dot_general(centered, centered, NT, preferred_element_type=F32)
    scaled = gram / (IMAGES - 1)
    ridged = scaled + RIDGE * eye
    parts = split(ridged)
    square = fine_dot(parts, parts)
    squares = jnp.sum(scaled * (scaled + (2.0 * RIDGE) * eye))
    frob = jnp.sqrt(squares + RIDGE * RIDGE * CH)
    inverse = 1.0 / frob
    u = ridged * inverse
    v = square * inverse * inverse
    high = fine_dot(split(v), split(0.0625 * v - 0.5625 * u))
    lower = (2.25 * eye - 2.4375 * u) + 1.6875 * v + high
    high, low = split(lower / jnp.sqrt(frob))
    white = jnp.dot(high, centered, preferred_element_type=F32)
    white = white + jnp.dot(low, centered, preferred_element_type=F32)
    for k in range(NX):
        turn_ref[k] = white[:, k * 128 : (k + 1) * 128]
        for xs in range(NX):
            rows_ref[pl.ds(xs * 128 + k, 32, stride=4), :] = turn_ref[k, pl.ds(xs, 32, stride=4), :]
    out_ref[...] = rows_ref[...].astype(BF16)


def smooth_body(white_ref, weight_ref, out_ref, pad_ref, rows_ref):
    pad_ref[0] = jnp.zeros((48, 128), F32)
    pad_ref[17] = jnp.zeros((48, 128), F32)
    pad_ref[:, 0:8] = jnp.zeros((18, 8, 128), F32)
    pad_ref[:, 40:48] = jnp.zeros((18, 8, 128), F32)
    pad_ref[1:17, 8:40, :] = white_ref[...].astype(F32).reshape(ROWS, 32, 128)
    for h in range(ROWS):
        total = None
        for t in range(9):
            a, b = t // 3, t % 3
            piece = pad_ref[h + a, 4 + 4 * b : 36 + 4 * b, :].reshape(4, 8, 128) * weight_ref[t]
            total = piece if total is None else total + piece
        rows_ref[h * 32 : (h + 1) * 32, :] = total.reshape(32, 128)
    for k in range(NX):
        out_ref[:, k * 128 : (k + 1) * 128] = rows_ref[pl.ds(k, 128, stride=4), :].astype(BF16)


def exchange(value, axes):
    return lax.all_to_all(value, axes, 0, 0, tiled=True)


def shards(backbone, conv_weight, smooth_weight):
    image = backbone.reshape(ROWS * COLS, CH)
    chunk = conv_weight.transpose(0, 1, 3, 2).reshape(9, 4, CH)
    group = NX * NZ
    spread = jnp.broadcast_to(image[None], (group,) + image.shape)
    images = exchange(spread, ("x", "z"))
    kernels = lax.all_gather(chunk, ("y", "c"))
    kernels, smooth_weight = lax.optimization_barrier((kernels, smooth_weight))
    taps = jnp.tile(smooth_weight.reshape(9, 4, 128), (1, 2, 1))
    features = vmem_call(
        conv_body,
        jax.ShapeDtypeStruct((512, 128), BF16),
        [
            pltpu.VMEM((640, CH), BF16),
            pltpu.VMEM((5, group, 160, 128), F32),
            pltpu.VMEM((512, 128), F32),
        ],
    )(kernels, images)
    features, taps = lax.optimization_barrier((features, taps))
    got = exchange(features.reshape(128, 4, 128), AXES)
    white = vmem_call(
        stats_body,
        jax.ShapeDtypeStruct((512, 128), BF16),
        [pltpu.VMEM((NX, 128, 128), F32), pltpu.VMEM((512, 128), F32)],
    )(got.reshape(512, 128))
    back = exchange(white.reshape(128, 4, 128), AXES)
    out = vmem_call(
        smooth_body,
        jax.ShapeDtypeStruct((128, CH), BF16),
        [pltpu.VMEM((18, 48, 128), F32), pltpu.VMEM((512, 128), F32)],
    )(back.reshape(512, 128), taps)
    return out.reshape(1, ROWS, COLS, CH)


def solution(mesh):
    split = Mesh(
        mesh.devices.reshape(NX, NZ, NY, NC, mesh.shape["rep"]), AXES + ("rep",)
    )
    whole = ("rep",) + AXES
    return jax.shard_map(
        shards,
        mesh=split,
        in_specs=(P(whole, None, None, None), P(None, None, None, whole), P(None, None, "rep")),
        out_specs=P(whole, None, None, None),
        check_vma=False,
    )
```
